128 devices in a mesh: stream: 16 (over y, x), azim: 8 (over z, core).
Axes of the slice: x: 4, y: 4, z: 4, core: 2. Of those that a mesh axis runs over, the one named last changes fastest.
Arguments:
- start_vector: bfloat16 [64, 8, 8, 64, 128], P('stream', 'azim'), may hold values from -6 to 6
- trace_blocks: bfloat16 [64, 8, 8, 64, 768], P('stream', 'azim'), may hold values from -0.21875 to 0.21875
- neighbour: int32 [8, 8, 12], P('azim'), may hold values from 0 to 71
Outputs:
- krylov_basis: bfloat16 [4, 64, 8, 8, 64, 128], P(None, 'stream', 'azim')
The draws below stay inside these ranges and needn't reach their ends.
Inputs may be any that keep to these rules, and one draw needn't show every extreme that they name: `neighbour`: entry e names column offsets (e // 24 - 1, (e // 8) % 3 - 1) and slot e % 8; the list is the same for every stream column.
All inputs are finite; a program needn't handle non-finite values.
Results may differ from the reference program's by a relative error of at most 0.0055.
Values may be sent and summed in bfloat16 or wider, within the bound.
A program may use at most 64 MiB of HBM per device.

```python
import jax
import jax.numpy as jnp
from jax import lax

FB = 64
NB = 12
STEPS = 4
C = 8
R = 128
NS = 64
NA = 8


def place_ends(drawn, own_key, low, top_value):
    longest = drawn.shape.index(max(drawn.shape))
    spots = []
    for shift in (0, 1):
        where = [jax.random.randint(jax.random.fold_in(own_key, axis), (), 0, length) for axis, length in enumerate(drawn.shape)]
        where[longest] = (where[longest] + shift) % drawn.shape[longest]
        spots.append(tuple(where))
    return drawn.at[spots[0]].set(low).at[spots[1]].set(top_value)


def shard_levels(own_key, dims, split, least, high):
    def one(dim, parts):
        draws = jax.random.uniform(jax.random.fold_in(jax.random.fold_in(own_key, 6), dim), (parts,), jnp.float32, least / len(split), high / len(split))
        return jnp.repeat(jnp.exp(draws), dims[dim] // parts).reshape((-1,) + (1,) * (len(dims) - dim - 1))

    level = one(*split[0])
    for cut in split[1:]:
        level = level * one(*cut)
    return level


def scatter_about(key, dims, deviation, bound, pieces=(), held_as=jnp.bfloat16):
    entries = jax.random.normal(key, dims, jnp.float32) * deviation
    if len(pieces) > 0:
        entries = shard_levels(key, dims, pieces, -0.22, 0.18) * entries
    return jnp.clip(entries, min=-bound, max=bound).astype(held_as)


def setup_inputs(seed: int = 0) -> dict:
    key_list = jax.random.split(jax.random.key(seed), 4)
    return {
        "start_vector": scatter_about(key_list[0], (NS, NA, C, FB, R), 1.0, 6.0, ((0, 16), (1, 8))),
        "trace_blocks": scatter_about(key_list[1], (NS, NA, C, FB, NB * FB), (NB * FB) ** -0.5, 0.21875, ((0, 16), (1, 8))),
        "neighbour": place_ends(jax.random.randint(key_list[2], (NA, C, NB), 0, 9 * C), jax.random.fold_in(key_list[2], 1), 0, (9 * C) - 1).astype(jnp.int32),
    }


def apply_rows(padded, blocks, neighbour, rows):
    column_count = padded.shape[1] - 2
    face_count = padded.shape[2]
    offset_code = neighbour // face_count
    slot_index = neighbour - offset_code * face_count
    stream_shift = offset_code // 3
    azim_shift = offset_code - stream_shift * 3
    row_index = jnp.arange(rows, dtype=jnp.int32)[:, None, None, None]
    column_index = jnp.arange(column_count, dtype=jnp.int32)[None, :, None, None]
    gathered = padded[row_index + stream_shift[None], column_index + azim_shift[None], slot_index[None]]
    gathered = gathered.reshape(rows, column_count, face_count, -1, padded.shape[-1])
    product = jnp.einsum("ijcam,ijcmr->ijcar", blocks.astype(jnp.float32), gathered.astype(jnp.float32))
    return product.astype(jnp.bfloat16)


def reference(start_vector, trace_blocks, neighbour):
    current = start_vector
    basis = []
    for layer_index in range(STEPS):
        wrapped = jnp.concatenate([current[-1:], current, current[:1]], axis=0)
        wrapped = jnp.concatenate([wrapped[:, -1:], wrapped, wrapped[:, :1]], axis=1)

        def one_column(position):
            window = lax.dynamic_slice_in_dim(wrapped, position, 3, 0)
            blocks = lax.dynamic_slice_in_dim(trace_blocks, position, 1, 0)
            return apply_rows(window, blocks, neighbour, 1)[0]

        current = lax.map(one_column, jnp.arange(NS, dtype=jnp.int32))
        basis.append(current)
    return jnp.stack(basis)
```

```python
import functools

import jax
import jax.numpy as jnp
from jax import lax
from jax.experimental import pallas as pl
from jax.experimental.pallas import tpu as pltpu
from jax.sharding import PartitionSpec as P

STEPS = 4
MESH = pl.DeviceIdType.MESH


def kernel(
    stream_count, azim_count, columns, faces, couplings,
    neighbour, start_hbm, blocks_hbm, out_hbm,
    vec, blocks, window, from_pair, from_far, from_line, pair_diag, far_diag,
    load_sem, out_sem, pair_s, pair_r, far_s, far_r, line_s, line_r, pd_s, pd_r, fd_s, fd_r,
):
    last = columns - 1
    half = faces // 2
    s = lax.axis_index("stream")
    j = lax.axis_index("azim")
    odd = lax.rem(j, 2)
    pair = {"azim": j + 1 - 2 * odd}
    far = {"azim": lax.rem(j + azim_count - 1 + 2 * odd, azim_count)}
    line = (
        {"stream": lax.rem(s + stream_count - 1, stream_count)},
        {"stream": lax.rem(s + 1, stream_count)},
    )
    pair_slot = 2 - 2 * odd
    far_slot = 2 * odd
    per_column = 3 * faces
    per_window = (columns + 2) * per_column

    load_start = pltpu.make_async_copy(start_hbm, vec.at[0], load_sem.at[0])
    load_blocks = pltpu.make_async_copy(blocks_hbm, blocks, load_sem.at[1])
    load_start.start()
    load_blocks.start()

    barrier = pltpu.get_barrier_semaphore()
    for target in (pair, far, *line):
        pl.semaphore_signal(barrier, inc=1, device_id=target, device_id_type=MESH)
    pl.semaphore_wait(barrier, 4)

    def remote(src, dst, send, recv, target):
        return pltpu.make_async_remote_copy(
            src_ref=src, dst_ref=dst, send_sem=send, recv_sem=recv, device_id=target, device_id_type=MESH
        )

    def far_copy(e, i, h):
        part = pl.ds(i * faces + h * half, half)
        return remote(vec.at[e, part], from_far.at[e, part], far_s.at[e, i, h], far_r.at[e, i, h], far)

    def pair_copy(e, i):
        part = pl.ds(i * faces, faces)
        return remote(vec.at[e, part], from_pair.at[e, part], pair_s.at[e, i], pair_r.at[e, i], pair)

    def line_copy(e, side):
        part = pl.ds(0 if side == 0 else last * faces, faces)
        there = 1 - side
        return remote(vec.at[e, part], from_line.at[e, there], line_s.at[e, there], line_r.at[e, there], line[side])

    def pair_relay(e, side):
        return remote(from_line.at[e, side], pair_diag.at[e, side], pd_s.at[e, side], pd_r.at[e, side], pair)

    def far_relay(e, side, h):
        i = 0 if side == 0 else last
        there = 1 - side
        return remote(
            from_far.at[e, pl.ds(i * faces + h * half, half)],
            far_diag.at[e, there, pl.ds(h * half, half)],
            fd_s.at[e, there, h],
            fd_r.at[e, there, h],
            line[side],
        )

    def fill(parity, position, slot, values):
        at = parity * per_window + position * per_column + slot * faces
        window[pl.ds(at, faces)] = values

    def compute(e, i):
        parity = lax.rem(e, 2)
        base = parity * per_window + i * per_column
        other = (1 - parity) * per_window + (i + 1) * per_column + faces
        for c in range(faces):
            gathered = jnp.concatenate(
                [window[base + neighbour[c * couplings + k]] for k in range(couplings)], axis=0
            )
            value = jnp.dot(
                blocks[i * faces + c], gathered, preferred_element_type=jnp.float32
            ).astype(jnp.bfloat16)
            vec[e + 1, i * faces + c] = value
            window[other + c] = value

    load_start.wait()
    for h in range(2):
        far_copy(0, 0, h).start()
        far_copy(0, last, h).start()
        if h == 0:
            for side in range(2):
                line_copy(0, side).start()
    pair_copy(0, 0).start()
    pair_copy(0, last).start()
    for i in range(1, last):
        for h in range(2):
            far_copy(0, i, h).start()
        pair_copy(0, i).start()
    for i in range(columns):
        fill(0, i + 1, 1, vec[0, pl.ds(i * faces, faces)])
    load_blocks.wait()

    def step(e, carry):
        parity = lax.rem(e, 2)
        more = e < STEPS - 1
        for h in range(2):
            for side in range(2):
                far_copy(e, 0 if side == 0 else last, h).wait_recv()
                far_relay(e, side, h).start()
        for side in range(2):
            line_copy(e, 1 - side).wait_recv()
            pair_relay(e, side).start()
        for i in range(columns):
            pair_copy(e, i).wait_recv()
            fill(parity, i + 1, pair_slot, from_pair[e, pl.ds(i * faces, faces)])
        for i in (0, last):
            fill(parity, i + 1, far_slot, from_far[e, pl.ds(i * faces, faces)])
        for side in range(2):
            fill(parity, side * (columns + 1), 1, from_line[e, side])
        for side in range(2):
            pair_relay(e, side).wait_recv()
            fill(parity, side * (columns + 1), pair_slot, pair_diag[e, side])
        for i in range(1, last):
            for h in range(2):
                far_copy(e, i, h).wait_recv()
            fill(parity, i + 1, far_slot, from_far[e, pl.ds(i * faces, faces)])
        for side in range(2):
            i = 0 if side == 0 else last
            for h in range(2):
                far_relay(e, 1 - side, h).wait_recv()
            fill(parity, side * (columns + 1), far_slot, far_diag[e, side])
            compute(e, i)

            @pl.when(more)
            def _():
                line_copy(e + 1, side).start()
                if side == 0:
                    far_copy(e + 1, 0, 0).start()
                else:
                    far_copy(e + 1, last, 0).start()
                    far_copy(e + 1, 0, 1).start()
                    far_copy(e + 1, last, 1).start()
                pair_copy(e + 1, i).start()

        for i in range(1, last):
            compute(e, i)

            @pl.when(more)
            def _():
                for h in range(2):
                    far_copy(e + 1, i, h).start()
                pair_copy(e + 1, i).start()

        pltpu.make_async_copy(vec.at[e + 1], out_hbm.at[e], out_sem.at[e]).start()
        return carry

    lax.fori_loop(0, STEPS, step, 0)

    def drain(e, carry):
        for i in range(columns):
            for h in range(2):
                far_copy(e, i, h).wait_send()
            pair_copy(e, i).wait_send()
        for side in range(2):
            line_copy(e, side).wait_send()
            pair_relay(e, side).wait_send()
            for h in range(2):
                far_relay(e, side, h).wait_send()
        pltpu.make_async_copy(vec.at[e + 1], out_hbm.at[e], out_sem.at[e]).wait()
        return carry

    lax.fori_loop(0, STEPS, drain, 0)


def solution(mesh):
    stream_count, azim_count = mesh.shape["stream"], mesh.shape["azim"]

    def local(start_vector, trace_blocks, neighbour):
        columns, _, faces, width, rhs = start_vector.shape
        depth = trace_blocks.shape[-1]
        couplings = neighbour.shape[-1]
        total = columns * faces
        slab = (width, rhs)
        bf16 = jnp.bfloat16
        dma = pltpu.SemaphoreType.DMA
        out = pl.pallas_call(
            functools.partial(kernel, stream_count, azim_count, columns, faces, couplings),
            out_shape=jax.ShapeDtypeStruct((STEPS, total, *slab), bf16),
            in_specs=[
                pl.BlockSpec(memory_space=pltpu.SMEM),
                pl.BlockSpec(memory_space=pl.ANY),
                pl.BlockSpec(memory_space=pl.ANY),
            ],
            out_specs=pl.BlockSpec(memory_space=pl.ANY),
            scratch_shapes=[
                pltpu.VMEM((STEPS + 1, total, *slab), bf16),
                pltpu.VMEM((total, width, depth), bf16),
                pltpu.VMEM((2 * (columns + 2) * 3 * faces, *slab), bf16),
                pltpu.VMEM((STEPS, total, *slab), bf16),
                pltpu.VMEM((STEPS, total, *slab), bf16),
                pltpu.VMEM((STEPS, 2, faces, *slab), bf16),
                pltpu.VMEM((STEPS, 2, faces, *slab), bf16),
                pltpu.VMEM((STEPS, 2, faces, *slab), bf16),
                dma((2,)),
                dma((STEPS,)),
                dma((STEPS, columns)),
                dma((STEPS, columns)),
                dma((STEPS, columns, 2)),
                dma((STEPS, columns, 2)),
                dma((STEPS, 2)),
                dma((STEPS, 2)),
                dma((STEPS, 2)),
                dma((STEPS, 2)),
                dma((STEPS, 2, 2)),
                dma((STEPS, 2, 2)),
            ],
            compiler_params=pltpu.CompilerParams(collective_id=0, has_side_effects=True),
        )(
            neighbour.reshape(-1),
            start_vector.reshape(total, *slab),
            trace_blocks.reshape(total, width, depth),
        )
        return out.reshape(STEPS, columns, 1, faces, *slab)

    return jax.shard_map(
        local,
        mesh=mesh,
        in_specs=(
            P("stream", "azim", None, None, None),
            P("stream", "azim", None, None, None),
            P("azim", None, None),
        ),
        out_specs=P(None, "stream", "azim", None, None, None),
        check_vma=False,
    )
```

```python
import functools

import jax
import jax.numpy as jnp
from jax import lax
from jax.experimental import pallas as pl
from jax.experimental.pallas import tpu as pltpu
from jax.sharding import PartitionSpec as P

STEPS = 4
ROW = 4
PARTS = 4
OPT = dict(H=2, order=1, N=4, OUT=2)
MESH = pl.DeviceIdType.MESH


def kernel(
    stream_count, azim_count, columns, faces, couplings,
    neighbour, start_hbm, blocks_hbm, out_hbm,
    vec, blocks, window, from_pair, from_far, from_line, pair_diag, far_diag,
    load_sem, out_sem, pair_s, pair_r, far_s, far_r, line_s, line_r, pd_s, pd_r, fd_s, fd_r,
):
    last = columns - 1
    parts = OPT['H']
    half = faces // parts
    s = lax.axis_index("stream")
    j = lax.axis_index("azim")
    odd = lax.rem(j, 2)
    pair = {"azim": j + 1 - 2 * odd}
    far = {"azim": lax.rem(j + azim_count - 1 + 2 * odd, azim_count)}

    def line(side):
        return {"stream": lax.rem(s + stream_count - 1 + 2 * side, stream_count)}

    first = lax.rem(s, ROW) // 2 if OPT['order'] else 0
    sides = (first, 1 - first)
    pair_slot = 2 - 2 * odd
    far_slot = 2 * odd
    per_column = 3 * faces
    per_window = (columns + 2) * per_column

    load_start = pltpu.make_async_copy(start_hbm, vec.at[0], load_sem.at[0])
    load_blocks = pltpu.make_async_copy(blocks_hbm, blocks, load_sem.at[1])
    load_start.start()
    load_blocks.start()

    barrier = pltpu.get_barrier_semaphore()
    for target in (pair, far, line(0), line(1)):
        pl.semaphore_signal(barrier, inc=1, device_id=target, device_id_type=MESH)
    pl.semaphore_wait(barrier, 4)

    def remote(src, dst, send, recv, target):
        return pltpu.make_async_remote_copy(
            src_ref=src, dst_ref=dst, send_sem=send, recv_sem=recv, device_id=target, device_id_type=MESH
        )

    def far_copy(e, i, h):
        part = pl.ds(i * faces + h * half, half)
        return remote(vec.at[e, part], from_far.at[e, part], far_s.at[e, i, h], far_r.at[e, i, h], far)

    def pair_copy(e, i):
        part = pl.ds(i * faces, faces)
        return remote(vec.at[e, part], from_pair.at[e, part], pair_s.at[e, i], pair_r.at[e, i], pair)

    def line_copy(e, side):
        part = pl.ds(side * last * faces, faces)
        there = 1 - side
        return remote(vec.at[e, part], from_line.at[e, there], line_s.at[e, there], line_r.at[e, there], line(side))

    def pair_relay(e, side):
        return remote(from_line.at[e, side], pair_diag.at[e, side], pd_s.at[e, side], pd_r.at[e, side], pair)

    def far_relay(e, side, h):
        i = side * last
        there = 1 - side
        return remote(
            from_far.at[e, pl.ds(i * faces + h * half, half)],
            far_diag.at[e, there, pl.ds(h * half, half)],
            fd_s.at[e, there, h],
            fd_r.at[e, there, h],
            line(side),
        )

    def fill(parity, position, slot, values):
        at = parity * per_window + position * per_column + slot * faces
        window[pl.ds(at, faces)] = values

    def compute(e, i):
        parity = lax.rem(e, 2)
        base = parity * per_window + i * per_column
        for c in range(faces):
            gathered = jnp.concatenate(
                [window[base + neighbour[0, c, k]] for k in range(couplings)], axis=0
            )
            value = jnp.dot(
                blocks[i * faces + c], gathered, preferred_element_type=jnp.float32
            ).astype(jnp.bfloat16)
            vec[e + 1, i * faces + c] = value
            if OPT['OUT']:
                out_hbm[e, i * faces + c] = value

    def send_edge(e, side):
        for h in range(parts):
            far_copy(e, side * last, h).start()
            if h == 0:
                line_copy(e, side).start()
                pair_copy(e, side * last).start()

    load_start.wait()
    for side in sides:
        send_edge(0, side)
    for i in range(1, last):
        for h in range(parts):
            far_copy(0, i, h).start()
        pair_copy(0, i).start()
    load_blocks.wait()

    def step(e, carry):
        parity = lax.rem(e, 2)
        more = e < OPT['N'] - 1
        for side in sides:
            for h in range(parts):
                far_copy(e, side * last, h).wait_recv()
                far_relay(e, side, h).start()
        for side in sides:
            line_copy(e, 1 - side).wait_recv()
            pair_relay(e, side).start()
        for i in range(columns):
            fill(parity, i + 1, 1, vec[e, pl.ds(i * faces, faces)])
        for i in range(columns):
            pair_copy(e, i).wait_recv()
            fill(parity, i + 1, pair_slot, from_pair[e, pl.ds(i * faces, faces)])
        for i in (0, last):
            fill(parity, i + 1, far_slot, from_far[e, pl.ds(i * faces, faces)])
        for side in range(2):
            fill(parity, side * (columns + 1), 1, from_line[e, side])
        for side in range(2):
            pair_relay(e, side).wait_recv()
            fill(parity, side * (columns + 1), pair_slot, pair_diag[e, side])
        for i in range(1, last):
            for h in range(parts):
                far_copy(e, i, h).wait_recv()
            fill(parity, i + 1, far_slot, from_far[e, pl.ds(i * faces, faces)])
        for side in sides:
            for h in range(parts):
                far_relay(e, 1 - side, h).wait_recv()
            fill(parity, side * (columns + 1), far_slot, far_diag[e, side])
            compute(e, side * last)

            @pl.when(more)
            def _():
                send_edge(e + 1, side)

        for i in range(1, last):
            compute(e, i)

            @pl.when(more)
            def _():
                for h in range(parts):
                    far_copy(e + 1, i, h).start()
                pair_copy(e + 1, i).start()

        if not OPT['OUT']:
            pltpu.make_async_copy(vec.at[e + 1], out_hbm.at[e], out_sem.at[e]).start()
        return carry

    lax.fori_loop(0, OPT['N'], step, 0)

    def drain(e, carry):
        for i in range(columns):
            for h in range(parts):
                far_copy(e, i, h).wait_send()
            pair_copy(e, i).wait_send()
        for side in range(2):
            line_copy(e, side).wait_send()
            pair_relay(e, side).wait_send()
            for h in range(parts):
                far_relay(e, side, h).wait_send()
        if not OPT['OUT']:
            pltpu.make_async_copy(vec.at[e + 1], out_hbm.at[e], out_sem.at[e]).wait()
        return carry

    lax.fori_loop(0, OPT['N'], drain, 0)


def solution(mesh):
    stream_count, azim_count = mesh.shape["stream"], mesh.shape["azim"]

    def local(start_vector, trace_blocks, neighbour):
        columns, _, faces, width, rhs = start_vector.shape
        depth = trace_blocks.shape[-1]
        couplings = neighbour.shape[-1]
        total = columns * faces
        slab = (width, rhs)
        bf16 = jnp.bfloat16
        dma = pltpu.SemaphoreType.DMA
        out = pl.pallas_call(
            functools.partial(kernel, stream_count, azim_count, columns, faces, couplings),
            out_shape=(pltpu.VMEM((STEPS, total, *slab), bf16) if OPT['OUT'] >= 2 else jax.ShapeDtypeStruct((STEPS, total, *slab), bf16)),
            in_specs=[
                pl.BlockSpec(memory_space=pltpu.SMEM),
                pl.BlockSpec(memory_space=pl.ANY),
                pl.BlockSpec(memory_space=pl.ANY),
            ],
            out_specs=pl.BlockSpec(memory_space=pltpu.VMEM if OPT['OUT'] else pl.ANY),
            scratch_shapes=[
                pltpu.VMEM((STEPS + 1, total, *slab), bf16),
                pltpu.VMEM((total, width, depth), bf16),
                pltpu.VMEM((2 * (columns + 2) * 3 * faces, *slab), bf16),
                pltpu.VMEM((STEPS, total, *slab), bf16),
                pltpu.VMEM((STEPS, total, *slab), bf16),
                pltpu.VMEM((STEPS, 2, faces, *slab), bf16),
                pltpu.VMEM((STEPS, 2, faces, *slab), bf16),
                pltpu.VMEM((STEPS, 2, faces, *slab), bf16),
                dma((2,)),
                dma((STEPS,)),
                dma((STEPS, columns)),
                dma((STEPS, columns)),
                dma((STEPS, columns, OPT['H'])),
                dma((STEPS, columns, OPT['H'])),
                dma((STEPS, 2)),
                dma((STEPS, 2)),
                dma((STEPS, 2)),
                dma((STEPS, 2)),
                dma((STEPS, 2, OPT['H'])),
                dma((STEPS, 2, OPT['H'])),
            ],
            compiler_params=pltpu.CompilerParams(collective_id=0, has_side_effects=True),
        )(
            neighbour,
            start_vector.reshape(total, *slab),
            trace_blocks.reshape(total, width, depth),
        )
        if OPT['OUT'] == 3:
            out = pltpu.with_memory_space_constraint(out, pltpu.VMEM)
        if OPT['OUT'] == 3:
            def put(x, o, sem):
                cs = [pltpu.make_async_copy(x.at[t], o.at[t], sem.at[t]) for t in range(STEPS)]
                for c in cs: c.start()
                for c in cs: c.wait()
            out = pl.pallas_call(put, out_shape=jax.ShapeDtypeStruct((STEPS, total, *slab), bf16),
                in_specs=[pl.BlockSpec(memory_space=pltpu.VMEM)], out_specs=pl.BlockSpec(memory_space=pl.ANY),
                scratch_shapes=[dma((STEPS,))])(out)
        return out.reshape(STEPS, columns, 1, faces, *slab)

    return jax.shard_map(
        local,
        mesh=mesh,
        in_specs=(
            P("stream", "azim", None, None, None),
            P("stream", "azim", None, None, None),
            P("azim", None, None),
        ),
        out_specs=P(None, "stream", "azim", None, None, None),
        check_vma=False,
    )
```

```python
import functools

import jax
import jax.numpy as jnp
from jax import lax
from jax.experimental import pallas as pl
from jax.experimental.pallas import tpu as pltpu
from jax.sharding import PartitionSpec as P

STEPS = 4
ROW = 4
MESH = pl.DeviceIdType.MESH
CUTS = (0, 3, 5)


def kernel(
    stream_count, azim_count, columns, faces, couplings, cuts,
    neighbour, start_hbm, blocks_hbm, out,
    vec, blocks, window, from_pair, from_far, from_line, pair_diag, far_diag,
    load_sem, pair_s, pair_r, far_s, far_r, line_s, line_r, pd_s, pd_r, fd_s, fd_r,
):
    parts = len(cuts) - 1
    last = columns - 1
    s = lax.axis_index("stream")
    j = lax.axis_index("azim")
    odd = lax.rem(j, 2)
    pair = {"azim": j + 1 - 2 * odd}
    far = {"azim": lax.rem(j + azim_count - 1 + 2 * odd, azim_count)}

    def line(side):
        return {"stream": lax.rem(s + stream_count - 1 + 2 * side, stream_count)}

    place = lax.rem(s, ROW)
    first = place // 2
    sides = (first, 1 - first)
    at_end = lax.rem(place, ROW - 1) == 0
    pair_slot = 2 - 2 * odd
    inner = (1 + first * (columns - 3), columns - 2 - first * (columns - 3))
    far_slot = 2 * odd
    per_column = 3 * faces
    per_window = (columns + 2) * per_column

    load_start = pltpu.make_async_copy(start_hbm, vec.at[0], load_sem.at[0])
    load_blocks = pltpu.make_async_copy(blocks_hbm, blocks, load_sem.at[1])
    load_start.start()

    barrier = pltpu.get_barrier_semaphore()
    for target in (pair, far, line(0), line(1)):
        pl.semaphore_signal(barrier, inc=1, device_id=target, device_id_type=MESH)
    pl.semaphore_wait(barrier, 4)

    def remote(src, dst, send, recv, target):
        return pltpu.make_async_remote_copy(
            src_ref=src, dst_ref=dst, send_sem=send, recv_sem=recv, device_id=target, device_id_type=MESH
        )

    def far_copy(e, i, h):
        part = pl.ds(i * faces + cuts[h], cuts[h + 1] - cuts[h])
        return remote(vec.at[e, part], from_far.at[e, part], far_s.at[e, i, h], far_r.at[e, i, h], far)

    def far_whole(e, i):
        part = pl.ds(i * faces, faces)
        return remote(vec.at[e, part], from_far.at[e, part], far_s.at[e, i, 0], far_r.at[e, i, 0], far)

    def pair_copy(e, i):
        part = pl.ds(i * faces, faces)
        return remote(vec.at[e, part], from_pair.at[e, part], pair_s.at[e, i], pair_r.at[e, i], pair)

    def line_copy(e, side, piece):
        begin, end = (cuts[-2], faces) if piece == 0 else (0, cuts[-2])
        there = 1 - side
        return remote(
            vec.at[e, pl.ds(side * last * faces + begin, end - begin)],
            from_line.at[e, there, pl.ds(begin, end - begin)],
            line_s.at[e, there, piece],
            line_r.at[e, there, piece],
            line(side),
        )

    def pair_relay(e, side):
        return remote(from_line.at[e, side], pair_diag.at[e, side], pd_s.at[e, side], pd_r.at[e, side], pair)

    def far_relay(e, side, h):
        there = 1 - side
        size = cuts[h + 1] - cuts[h]
        return remote(
            from_far.at[e, pl.ds(side * last * faces + cuts[h], size)],
            far_diag.at[e, there, pl.ds(cuts[h], size)],
            fd_s.at[e, there, h],
            fd_r.at[e, there, h],
            line(side),
        )

    def end_relay(e, side):
        h = parts - 1
        part = pl.ds(cuts[h], cuts[h + 1] - cuts[h])
        return remote(
            from_line.at[e, side, part],
            far_diag.at[e, side, part],
            fd_s.at[e, 1 - side, h],
            fd_r.at[e, side, h],
            far,
        )

    def send_edge(e, side):
        for h in range(parts):
            far_copy(e, side * last, h).start()
            if h == 0:
                line_copy(e, side, 0).start()
                line_copy(e, side, 1).start()
                pair_copy(e, side * last).start()

    def send_inner(e, i):
        far_whole(e, i).start()
        pair_copy(e, i).start()

    def fill(parity, position, slot, values):
        at = parity * per_window + position * per_column + slot * faces
        window[pl.ds(at, faces)] = values

    def compute(e, i):
        base = lax.rem(e, 2) * per_window + i * per_column
        for c in range(faces):
            f = i * faces + c
            gathered = jnp.concatenate(
                [window[base + neighbour[0, c, k]] for k in range(couplings)], axis=0
            )
            value = jnp.dot(
                blocks[f], gathered, preferred_element_type=jnp.float32
            ).astype(jnp.bfloat16)
            vec[e + 1, f] = value
            out[e, f] = value

    load_start.wait()
    load_blocks.start()
    for side in sides:
        send_edge(0, side)
    for i in inner:
        send_inner(0, i)
    load_blocks.wait()

    def step(e, final):
        parity = lax.rem(e, 2)
        for n, side in enumerate(sides):
            for h in range(parts):
                far_copy(e, side * last, h).wait_recv()
                if n == 0 and h == parts - 1:

                    @pl.when(jnp.logical_not(at_end))
                    def _():
                        far_relay(e, side, h).start()

                else:
                    far_relay(e, side, h).start()
            if n == 0:
                line_copy(e, 1 - sides[0], 0).wait_recv()

                @pl.when(at_end)
                def _():
                    end_relay(e, sides[0]).start()

        for n in (1, 0):
            side = sides[n]
            if n == 1:
                line_copy(e, 1 - side, 0).wait_recv()
            line_copy(e, 1 - side, 1).wait_recv()
            pair_relay(e, side).start()
        for i in range(columns):
            fill(parity, i + 1, 1, vec[e, pl.ds(i * faces, faces)])
        for i in range(columns):
            pair_copy(e, i).wait_recv()
            fill(parity, i + 1, pair_slot, from_pair[e, pl.ds(i * faces, faces)])
        for i in (0, last):
            fill(parity, i + 1, far_slot, from_far[e, pl.ds(i * faces, faces)])
        for side in range(2):
            fill(parity, side * (columns + 1), 1, from_line[e, side])
        for i in inner:
            far_whole(e, i).wait_recv()
            fill(parity, i + 1, far_slot, from_far[e, pl.ds(i * faces, faces)])
        if final:
            for i in inner:
                compute(e, i)
        for side in range(2):
            pair_relay(e, side).wait_recv()
            fill(parity, side * (columns + 1), pair_slot, pair_diag[e, side])
        for side in sides:
            for h in range(parts):
                far_relay(e, 1 - side, h).wait_recv()
            fill(parity, side * (columns + 1), far_slot, far_diag[e, side])
            compute(e, side * last)
            if not final:
                send_edge(e + 1, side)
        if not final:
            for i in inner:
                compute(e, i)
                send_inner(e + 1, i)

    def middle(e, carry):
        step(e, False)
        return carry

    lax.fori_loop(0, STEPS - 1, middle, 0)
    step(STEPS - 1, True)

    def drain(e, carry):
        for i in range(columns):
            pair_copy(e, i).wait_send()
        for i in inner:
            far_whole(e, i).wait_send()
        for side in range(2):
            for piece in range(2):
                line_copy(e, side, piece).wait_send()
            pair_relay(e, side).wait_send()
            for h in range(parts):
                far_copy(e, side * last, h).wait_send()
                far_relay(e, side, h).wait_send()
        return carry

    lax.fori_loop(0, STEPS, drain, 0)


def solution(mesh):
    stream_count, azim_count = mesh.shape["stream"], mesh.shape["azim"]

    def local(start_vector, trace_blocks, neighbour):
        columns, _, faces, width, rhs = start_vector.shape
        depth = trace_blocks.shape[-1]
        couplings = neighbour.shape[-1]
        total = columns * faces
        slab = (width, rhs)
        bf16 = jnp.bfloat16
        dma = pltpu.SemaphoreType.DMA
        cuts = (*CUTS, faces)
        parts = len(cuts) - 1
        out = pl.pallas_call(
            functools.partial(kernel, stream_count, azim_count, columns, faces, couplings, cuts),
            out_shape=pltpu.VMEM((STEPS, total, *slab), bf16),
            in_specs=[
                pl.BlockSpec(memory_space=pltpu.SMEM),
                pl.BlockSpec(memory_space=pl.ANY),
                pl.BlockSpec(memory_space=pl.ANY),
            ],
            out_specs=pl.BlockSpec(memory_space=pltpu.VMEM),
            scratch_shapes=[
                pltpu.VMEM((STEPS + 1, total, *slab), bf16),
                pltpu.VMEM((total, width, depth), bf16),
                pltpu.VMEM((2 * (columns + 2) * 3 * faces, *slab), bf16),
                pltpu.VMEM((STEPS, total, *slab), bf16),
                pltpu.VMEM((STEPS, total, *slab), bf16),
                pltpu.VMEM((STEPS, 2, faces, *slab), bf16),
                pltpu.VMEM((STEPS, 2, faces, *slab), bf16),
                pltpu.VMEM((STEPS, 2, faces, *slab), bf16),
                dma((2,)),
                dma((STEPS, columns)),
                dma((STEPS, columns)),
                dma((STEPS, columns, parts)),
                dma((STEPS, columns, parts)),
                dma((STEPS, 2, 2)),
                dma((STEPS, 2, 2)),
                dma((STEPS, 2)),
                dma((STEPS, 2)),
                dma((STEPS, 2, parts)),
                dma((STEPS, 2, parts)),
            ],
            compiler_params=pltpu.CompilerParams(collective_id=0, has_side_effects=True),
        )(
            neighbour,
            start_vector.reshape(total, *slab),
            trace_blocks.reshape(total, width, depth),
        )
        return out.reshape(STEPS, columns, 1, faces, *slab)

    return jax.shard_map(
        local,
        mesh=mesh,
        in_specs=(
            P("stream", "azim", None, None, None),
            P("stream", "azim", None, None, None),
            P("azim", None, None),
        ),
        out_specs=P(None, "stream", "azim", None, None, None),
        check_vma=False,
    )
```

```python
import functools

import jax
import jax.numpy as jnp
from jax import lax
from jax.experimental import pallas as pl
from jax.experimental.pallas import tpu as pltpu
from jax.sharding import PartitionSpec as P

STEPS = 4
ROW = 4
MESH = pl.DeviceIdType.MESH
CUTS = (0, 3, 5)


def kernel(
    stream_count, azim_count, columns, faces, couplings, cuts,
    neighbour, start_hbm, blocks_hbm, out,
    vec, blocks, window, from_pair, from_far, from_line, pair_diag, far_diag,
    load_sem, pair_s, pair_r, far_s, far_r, line_s, line_r, pd_s, pd_r, fd_s, fd_r,
):
    parts = len(cuts) - 1
    last = columns - 1
    s = lax.axis_index("stream")
    j = lax.axis_index("azim")
    odd = lax.rem(j, 2)
    pair = {"azim": j + 1 - 2 * odd}
    far = {"azim": lax.rem(j + azim_count - 1 + 2 * odd, azim_count)}

    def line(side):
        return {"stream": lax.rem(s + stream_count - 1 + 2 * side, stream_count)}

    place = lax.rem(s, ROW)
    first = place // 2
    sides = (first, 1 - first)
    at_end = lax.rem(place, ROW - 1) == 0
    pair_slot = 2 - 2 * odd
    inner = (1 + first * (columns - 3), columns - 2 - first * (columns - 3))
    far_slot = 2 * odd
    per_column = 3 * faces
    per_window = (columns + 2) * per_column

    load_start = pltpu.make_async_copy(start_hbm, vec.at[0], load_sem.at[0])
    load_blocks = pltpu.make_async_copy(blocks_hbm, blocks, load_sem.at[1])
    load_start.start()

    barrier = pltpu.get_barrier_semaphore()
    for target in (pair, far, line(0), line(1)):
        pl.semaphore_signal(barrier, inc=1, device_id=target, device_id_type=MESH)
    pl.semaphore_wait(barrier, 4)

    def remote(src, dst, send, recv, target):
        return pltpu.make_async_remote_copy(
            src_ref=src, dst_ref=dst, send_sem=send, recv_sem=recv, device_id=target, device_id_type=MESH
        )

    def far_copy(e, i, h):
        part = pl.ds(i * faces + cuts[h], cuts[h + 1] - cuts[h])
        return remote(vec.at[e, part], from_far.at[e, part], far_s.at[e, i, h], far_r.at[e, i, h], far)

    def far_whole(e, i):
        part = pl.ds(i * faces, faces)
        return remote(vec.at[e, part], from_far.at[e, part], far_s.at[e, i, 0], far_r.at[e, i, 0], far)

    def pair_copy(e, i):
        part = pl.ds(i * faces, faces)
        return remote(vec.at[e, part], from_pair.at[e, part], pair_s.at[e, i], pair_r.at[e, i], pair)

    def line_copy(e, side, piece):
        begin, end = (cuts[-2], faces) if piece == 0 else (0, cuts[-2])
        there = 1 - side
        return remote(
            vec.at[e, pl.ds(side * last * faces + begin, end - begin)],
            from_line.at[e, there, pl.ds(begin, end - begin)],
            line_s.at[e, there, piece],
            line_r.at[e, there, piece],
            line(side),
        )

    def pair_relay(e, side):
        return remote(from_line.at[e, side], pair_diag.at[e, side], pd_s.at[e, side], pd_r.at[e, side], pair)

    def far_relay(e, side, h):
        there = 1 - side
        size = cuts[h + 1] - cuts[h]
        return remote(
            from_far.at[e, pl.ds(side * last * faces + cuts[h], size)],
            far_diag.at[e, there, pl.ds(cuts[h], size)],
            fd_s.at[e, there, h],
            fd_r.at[e, there, h],
            line(side),
        )

    def end_relay(e, side):
        h = parts - 1
        part = pl.ds(cuts[h], cuts[h + 1] - cuts[h])
        return remote(
            from_line.at[e, side, part],
            far_diag.at[e, side, part],
            fd_s.at[e, 1 - side, h],
            fd_r.at[e, side, h],
            far,
        )

    def send_edge(e, side):
        line_copy(e, side, 0).start()
        for h in range(parts):
            far_copy(e, side * last, h).start()
            if h == 0:
                line_copy(e, side, 1).start()
                pair_copy(e, side * last).start()

    def send_inner(e, i):
        far_whole(e, i).start()
        pair_copy(e, i).start()

    def fill(parity, position, slot, values):
        at = parity * per_window + position * per_column + slot * faces
        window[pl.ds(at, faces)] = values

    def compute(e, i):
        base = lax.rem(e, 2) * per_window + i * per_column
        for c in range(faces):
            f = i * faces + c
            gathered = jnp.concatenate(
                [window[base + neighbour[0, c, k]] for k in range(couplings)], axis=0
            )
            value = jnp.dot(
                blocks[f], gathered, preferred_element_type=jnp.float32
            ).astype(jnp.bfloat16)
            vec[e + 1, f] = value
            out[e, f] = value

    load_start.wait()
    load_blocks.start()
    for side in sides:
        send_edge(0, side)
    for i in inner:
        send_inner(0, i)
    load_blocks.wait()

    def step(e, final):
        parity = lax.rem(e, 2)
        for n, side in enumerate(sides):
            for h in range(parts):
                far_copy(e, side * last, h).wait_recv()
                if n == 0 and h == parts - 1:

                    @pl.when(jnp.logical_not(at_end))
                    def _():
                        far_relay(e, side, h).start()

                else:
                    far_relay(e, side, h).start()
            if n == 0:
                line_copy(e, 1 - sides[0], 0).wait_recv()

                @pl.when(at_end)
                def _():
                    end_relay(e, sides[0]).start()

        for n in (1, 0):
            side = sides[n]
            if n == 1:
                line_copy(e, 1 - side, 0).wait_recv()
            line_copy(e, 1 - side, 1).wait_recv()
            pair_relay(e, side).start()
        for i in range(columns):
            fill(parity, i + 1, 1, vec[e, pl.ds(i * faces, faces)])
        for i in range(columns):
            pair_copy(e, i).wait_recv()
            fill(parity, i + 1, pair_slot, from_pair[e, pl.ds(i * faces, faces)])
        for i in (0, last):
            fill(parity, i + 1, far_slot, from_far[e, pl.ds(i * faces, faces)])
        for side in range(2):
            fill(parity, side * (columns + 1), 1, from_line[e, side])
        for i in inner:
            far_whole(e, i).wait_recv()
            fill(parity, i + 1, far_slot, from_far[e, pl.ds(i * faces, faces)])
        if final:
            for i in inner:
                compute(e, i)
        for side in range(2):
            pair_relay(e, side).wait_recv()
            fill(parity, side * (columns + 1), pair_slot, pair_diag[e, side])
        for side in sides:
            for h in range(parts):
                far_relay(e, 1 - side, h).wait_recv()
            fill(parity, side * (columns + 1), far_slot, far_diag[e, side])
            compute(e, side * last)
            if not final:
                send_edge(e + 1, side)
        if not final:
            for i in inner:
                compute(e, i)
                send_inner(e + 1, i)

    def middle(e, carry):
        step(e, False)
        return carry

    lax.fori_loop(0, STEPS - 1, middle, 0)
    step(STEPS - 1, True)

    def drain(e, carry):
        for i in range(columns):
            pair_copy(e, i).wait_send()
        for i in inner:
            far_whole(e, i).wait_send()
        for side in range(2):
            for piece in range(2):
                line_copy(e, side, piece).wait_send()
            pair_relay(e, side).wait_send()
            for h in range(parts):
                far_copy(e, side * last, h).wait_send()
                far_relay(e, side, h).wait_send()
        return carry

    lax.fori_loop(0, STEPS, drain, 0)


def solution(mesh):
    stream_count, azim_count = mesh.shape["stream"], mesh.shape["azim"]

    def local(start_vector, trace_blocks, neighbour):
        columns, _, faces, width, rhs = start_vector.shape
        depth = trace_blocks.shape[-1]
        couplings = neighbour.shape[-1]
        total = columns * faces
        slab = (width, rhs)
        bf16 = jnp.bfloat16
        dma = pltpu.SemaphoreType.DMA
        cuts = (*CUTS, faces)
        parts = len(cuts) - 1
        out = pl.pallas_call(
            functools.partial(kernel, stream_count, azim_count, columns, faces, couplings, cuts),
            out_shape=pltpu.VMEM((STEPS, total, *slab), bf16),
            in_specs=[
                pl.BlockSpec(memory_space=pltpu.SMEM),
                pl.BlockSpec(memory_space=pl.ANY),
                pl.BlockSpec(memory_space=pl.ANY),
            ],
            out_specs=pl.BlockSpec(memory_space=pltpu.VMEM),
            scratch_shapes=[
                pltpu.VMEM((STEPS + 1, total, *slab), bf16),
                pltpu.VMEM((total, width, depth), bf16),
                pltpu.VMEM((2 * (columns + 2) * 3 * faces, *slab), bf16),
                pltpu.VMEM((STEPS, total, *slab), bf16),
                pltpu.VMEM((STEPS, total, *slab), bf16),
                pltpu.VMEM((STEPS, 2, faces, *slab), bf16),
                pltpu.VMEM((STEPS, 2, faces, *slab), bf16),
                pltpu.VMEM((STEPS, 2, faces, *slab), bf16),
                dma((2,)),
                dma((STEPS, columns)),
                dma((STEPS, columns)),
                dma((STEPS, columns, parts)),
                dma((STEPS, columns, parts)),
                dma((STEPS, 2, 2)),
                dma((STEPS, 2, 2)),
                dma((STEPS, 2)),
                dma((STEPS, 2)),
                dma((STEPS, 2, parts)),
                dma((STEPS, 2, parts)),
            ],
            compiler_params=pltpu.CompilerParams(
                collective_id=0,
                has_side_effects=True,
            ),
        )(
            neighbour,
            start_vector.reshape(total, *slab),
            trace_blocks.reshape(total, width, depth),
        )
        return out.reshape(STEPS, columns, 1, faces, *slab)

    return jax.shard_map(
        local,
        mesh=mesh,
        in_specs=(
            P("stream", "azim", None, None, None),
            P("stream", "azim", None, None, None),
            P("azim", None, None),
        ),
        out_specs=P(None, "stream", "azim", None, None, None),
        check_vma=False,
    )
```

```python
import functools

import jax
import jax.numpy as jnp
from jax import lax
from jax.experimental import pallas as pl
from jax.experimental.pallas import tpu as pltpu
from jax.sharding import PartitionSpec as P

STEPS = 4
ROW = 4
MESH = pl.DeviceIdType.MESH
CUTS = (0, 2, 5)


def kernel(
    stream_count, azim_count, columns, faces, couplings, cuts,
    neighbour, start_hbm, blocks_hbm, out,
    vec, blocks, window, from_pair, from_far, from_line, pair_diag, far_diag,
    load_sem, pair_s, pair_r, far_s, far_r, line_s, line_r, pd_s, pd_r, fd_s, fd_r,
):
    parts = len(cuts) - 1
    last = columns - 1
    s = lax.axis_index("stream")
    j = lax.axis_index("azim")
    odd = lax.rem(j, 2)
    pair = {"azim": j + 1 - 2 * odd}
    far = {"azim": lax.rem(j + azim_count - 1 + 2 * odd, azim_count)}

    def line(side):
        return {"stream": lax.rem(s + stream_count - 1 + 2 * side, stream_count)}

    place = lax.rem(s, ROW)
    first = place // 2
    sides = (first, 1 - first)
    at_end = lax.rem(place, ROW - 1) == 0
    pair_slot = 2 - 2 * odd
    inner = (1 + first * (columns - 3), columns - 2 - first * (columns - 3))
    far_slot = 2 * odd
    per_column = 3 * faces
    per_window = (columns + 2) * per_column

    load_start = pltpu.make_async_copy(start_hbm, vec.at[0], load_sem.at[0])
    load_blocks = pltpu.make_async_copy(blocks_hbm, blocks, load_sem.at[1])
    load_start.start()

    barrier = pltpu.get_barrier_semaphore()
    for target in (pair, far, line(0), line(1)):
        pl.semaphore_signal(barrier, inc=1, device_id=target, device_id_type=MESH)
    pl.semaphore_wait(barrier, 4)

    def remote(src, dst, send, recv, target):
        return pltpu.make_async_remote_copy(
            src_ref=src, dst_ref=dst, send_sem=send, recv_sem=recv, device_id=target, device_id_type=MESH
        )

    def far_copy(e, i, h):
        part = pl.ds(i * faces + cuts[h], cuts[h + 1] - cuts[h])
        return remote(vec.at[e, part], from_far.at[e, part], far_s.at[e, i, h], far_r.at[e, i, h], far)

    def far_whole(e, i):
        part = pl.ds(i * faces, faces)
        return remote(vec.at[e, part], from_far.at[e, part], far_s.at[e, i, 0], far_r.at[e, i, 0], far)

    def pair_copy(e, i):
        part = pl.ds(i * faces, faces)
        return remote(vec.at[e, part], from_pair.at[e, part], pair_s.at[e, i], pair_r.at[e, i], pair)

    def line_copy(e, side, piece):
        begin, end = (cuts[-2], faces) if piece == 0 else (0, cuts[-2])
        there = 1 - side
        return remote(
            vec.at[e, pl.ds(side * last * faces + begin, end - begin)],
            from_line.at[e, there, pl.ds(begin, end - begin)],
            line_s.at[e, there, piece],
            line_r.at[e, there, piece],
            line(side),
        )

    def pair_relay(e, side):
        return remote(from_line.at[e, side], pair_diag.at[e, side], pd_s.at[e, side], pd_r.at[e, side], pair)

    def far_relay(e, side, h):
        there = 1 - side
        size = cuts[h + 1] - cuts[h]
        return remote(
            from_far.at[e, pl.ds(side * last * faces + cuts[h], size)],
            far_diag.at[e, there, pl.ds(cuts[h], size)],
            fd_s.at[e, there, h],
            fd_r.at[e, there, h],
            line(side),
        )

    def end_relay(e, side):
        h = parts - 1
        part = pl.ds(cuts[h], cuts[h + 1] - cuts[h])
        return remote(
            from_line.at[e, side, part],
            far_diag.at[e, side, part],
            fd_s.at[e, 1 - side, h],
            fd_r.at[e, side, h],
            far,
        )

    def send_edge(e, side):
        line_copy(e, side, 0).start()
        for h in range(parts):
            far_copy(e, side * last, h).start()
            if h == 0:
                line_copy(e, side, 1).start()
                pair_copy(e, side * last).start()

    def send_inner(e, i):
        far_whole(e, i).start()
        pair_copy(e, i).start()

    def fill(parity, position, slot, values):
        at = parity * per_window + position * per_column + slot * faces
        window[pl.ds(at, faces)] = values

    def compute(e, i):
        base = lax.rem(e, 2) * per_window + i * per_column
        for c in range(faces):
            f = i * faces + c
            gathered = jnp.concatenate(
                [window[base + neighbour[0, c, k]] for k in range(couplings)], axis=0
            )
            value = jnp.dot(
                blocks[f], gathered, preferred_element_type=jnp.float32
            ).astype(jnp.bfloat16)
            vec[e + 1, f] = value
            out[e, f] = value

    load_start.wait()
    load_blocks.start()
    for side in sides:
        send_edge(0, side)
    for i in inner:
        send_inner(0, i)
    load_blocks.wait()

    def step(e, final):
        parity = lax.rem(e, 2)
        for n, side in enumerate(sides):
            for h in range(parts):
                far_copy(e, side * last, h).wait_recv()
                if n == 0 and h == parts - 1:

                    @pl.when(jnp.logical_not(at_end))
                    def _():
                        far_relay(e, side, h).start()

                else:
                    far_relay(e, side, h).start()
            if n == 0:
                line_copy(e, 1 - sides[0], 0).wait_recv()

                @pl.when(at_end)
                def _():
                    end_relay(e, sides[0]).start()

        for n in (1, 0):
            side = sides[n]
            if n == 1:
                line_copy(e, 1 - side, 0).wait_recv()
            line_copy(e, 1 - side, 1).wait_recv()
            pair_relay(e, side).start()
        for i in range(columns):
            fill(parity, i + 1, 1, vec[e, pl.ds(i * faces, faces)])
        for i in range(columns):
            pair_copy(e, i).wait_recv()
            fill(parity, i + 1, pair_slot, from_pair[e, pl.ds(i * faces, faces)])
        for i in (0, last):
            fill(parity, i + 1, far_slot, from_far[e, pl.ds(i * faces, faces)])
        for side in range(2):
            fill(parity, side * (columns + 1), 1, from_line[e, side])
        for i in inner:
            far_whole(e, i).wait_recv()
            fill(parity, i + 1, far_slot, from_far[e, pl.ds(i * faces, faces)])
        if final:
            for i in inner:
                compute(e, i)
        for side in range(2):
            pair_relay(e, side).wait_recv()
            fill(parity, side * (columns + 1), pair_slot, pair_diag[e, side])
        for side in sides:
            for h in range(parts):
                far_relay(e, 1 - side, h).wait_recv()
            fill(parity, side * (columns + 1), far_slot, far_diag[e, side])
            compute(e, side * last)
            if not final:
                send_edge(e + 1, side)
        if not final:
            for i in inner:
                compute(e, i)
                send_inner(e + 1, i)

    def middle(e, carry):
        step(e, False)
        return carry

    lax.fori_loop(0, STEPS - 1, middle, 0)
    step(STEPS - 1, True)

    def drain(e, carry):
        for i in range(columns):
            pair_copy(e, i).wait_send()
        for i in inner:
            far_whole(e, i).wait_send()
        for side in range(2):
            for piece in range(2):
                line_copy(e, side, piece).wait_send()
            pair_relay(e, side).wait_send()
            for h in range(parts):
                far_copy(e, side * last, h).wait_send()
                far_relay(e, side, h).wait_send()
        return carry

    lax.fori_loop(0, STEPS, drain, 0)


def solution(mesh):
    stream_count, azim_count = mesh.shape["stream"], mesh.shape["azim"]

    def local(start_vector, trace_blocks, neighbour):
        columns, _, faces, width, rhs = start_vector.shape
        depth = trace_blocks.shape[-1]
        couplings = neighbour.shape[-1]
        total = columns * faces
        slab = (width, rhs)
        bf16 = jnp.bfloat16
        dma = pltpu.SemaphoreType.DMA
        cuts = (*CUTS, faces)
        parts = len(cuts) - 1
        out = pl.pallas_call(
            functools.partial(kernel, stream_count, azim_count, columns, faces, couplings, cuts),
            out_shape=pltpu.VMEM((STEPS, total, *slab), bf16),
            in_specs=[
                pl.BlockSpec(memory_space=pltpu.SMEM),
                pl.BlockSpec(memory_space=pl.ANY),
                pl.BlockSpec(memory_space=pl.ANY),
            ],
            out_specs=pl.BlockSpec(memory_space=pltpu.VMEM),
            scratch_shapes=[
                pltpu.VMEM((STEPS + 1, total, *slab), bf16),
                pltpu.VMEM((total, width, depth), bf16),
                pltpu.VMEM((2 * (columns + 2) * 3 * faces, *slab), bf16),
                pltpu.VMEM((STEPS, total, *slab), bf16),
                pltpu.VMEM((STEPS, total, *slab), bf16),
                pltpu.VMEM((STEPS, 2, faces, *slab), bf16),
                pltpu.VMEM((STEPS, 2, faces, *slab), bf16),
                pltpu.VMEM((STEPS, 2, faces, *slab), bf16),
                dma((2,)),
                dma((STEPS, columns)),
                dma((STEPS, columns)),
                dma((STEPS, columns, parts)),
                dma((STEPS, columns, parts)),
                dma((STEPS, 2, 2)),
                dma((STEPS, 2, 2)),
                dma((STEPS, 2)),
                dma((STEPS, 2)),
                dma((STEPS, 2, parts)),
                dma((STEPS, 2, parts)),
            ],
            compiler_params=pltpu.CompilerParams(
                collective_id=0,
                has_side_effects=True,
            ),
        )(
            neighbour,
            start_vector.reshape(total, *slab),
            trace_blocks.reshape(total, width, depth),
        )
        return out.reshape(STEPS, columns, 1, faces, *slab)

    return jax.shard_map(
        local,
        mesh=mesh,
        in_specs=(
            P("stream", "azim", None, None, None),
            P("stream", "azim", None, None, None),
            P("azim", None, None),
        ),
        out_specs=P(None, "stream", "azim", None, None, None),
        check_vma=False,
    )
```
